256 devices in a mesh: row: 32 (over z, x), col: 8 (over y, core).
Axes of the slice: x: 4, y: 4, z: 8, core: 2. Of those that a mesh axis runs over, the one named last changes fastest.
Arguments:
- right_side: float32 [15, 512, 512], P(None, 'row'), may hold values from -6 to 6
- off_blocks: float32 [8, 512, 2176], P('col', 'row'), may hold values from -0.09375 to 0.09375
- diag_inverse: float32 [8, 512, 960], P('col', 'row'), as said below
Outputs:
- forward_solution: float32 [8, 960, 512], P('col')
- solution: float32 [8, 4, 512, 512], P('col', None, 'row')
The draws below stay inside these ranges and needn't reach their ends.
Inputs may be any that keep to these rules, and one draw needn't show every extreme that they name: `diag_inverse`: read through the block map of the first step, each block D(n) is lower triangular with a positive diagonal between 0.5 and 2.
All inputs are finite; a program needn't handle non-finite values.
Results may differ from the reference program's by a relative error of at most 0.00011.
Values sent between devices are 32-bit elements; how exact they have to be, the bound alone decides.
No kernel may reach another device: no remote copies, remote signals or barrier semaphores. Data moves between devices by JAX's collectives and lax.ppermute only.
A program may use at most 64 MiB of HBM per device.

```python
import math
import jax
import jax.numpy as jnp
from jax import lax

W = 512
R = 512
LEVELS = 4
NODES = 15
GRID_COLS = 8
PAIR_SLAB = 2176
N_COL = 8


def row_index(width):
    return jnp.broadcast_to(jnp.arange(width, dtype=jnp.int32)[:, None], (width, width))


def draw_diag_inverse(key, part):
    first_key, second_key = jax.random.split(key)
    diagonal = jnp.exp(jax.random.uniform(first_key, (NODES, W), jnp.float32, math.log(0.5), math.log(2.0)))
    lower = jnp.clip(jax.random.normal(second_key, (NODES, W, W), jnp.float32), -6.0, 6.0) * (0.5 / math.sqrt(W))
    rows = row_index(W)
    cols = jnp.transpose(rows)
    natural = jnp.where((rows > cols)[None], lower, 0.0) + jnp.where((rows == cols)[None], diagonal[:, :, None], 0.0)
    packed = []
    for level in range(LEVELS):
        count = 2 ** level
        group = N_COL // count
        width = W // group
        blocks = natural[count - 1:2 * count - 1].reshape(count, group, width, W)
        packed.append(jnp.transpose(blocks, (0, 1, 3, 2)).reshape(N_COL, W, width))
    return jnp.concatenate(packed, axis=2)


def steps_of(rng, extent, shards, low, high):
    factor_of = 1.0
    for axis_at, shards_of in shards:
        heights = jax.random.uniform(jax.random.fold_in(jax.random.fold_in(rng, 6), axis_at), (shards_of,), jnp.float32, low / len(shards), high / len(shards))
        factor_of = factor_of * jnp.repeat(jnp.exp(heights), extent[axis_at] // shards_of).reshape((-1,) + (1,) * (len(extent) - 1 - axis_at))
    return factor_of


def bell_draw(key, extent, scale, most, cuts=(), kind=jnp.bfloat16):
    array = scale * jax.random.normal(key, extent, jnp.float32)
    if cuts:
        array = array * steps_of(key, extent, cuts, -0.22, 0.18)
    return jnp.clip(array, -most, most).astype(kind)


def setup_inputs(seed: int = 0) -> dict:
    seeds = jax.random.split(jax.random.key(seed), 4)
    right_side = bell_draw(seeds[0], (NODES, W, R), 1.0, 6.0, ((1, 32),), jnp.float32)
    off_blocks = bell_draw(seeds[1], (GRID_COLS, W, PAIR_SLAB), (8 * W) ** -0.5, 0.09375, ((0, 8), (1, 32)), jnp.float32)
    diag_inverse = draw_diag_inverse(jax.random.fold_in(seeds[3], 71), 0)
    return dict(right_side=right_side, off_blocks=off_blocks, diag_inverse=diag_inverse)


def pair_start(depth_down, depth_up):
    return (depth_down - 2) * 2 ** depth_down + 2 + depth_up * 2 ** depth_down


def unpack_diag(packed, depth_now):
    count = 2 ** depth_now
    group = N_COL // count
    width = W // group
    start = (count - 1) * W // N_COL
    piece = packed[:, :, start:start + width].reshape(count, group, W, width)
    return jnp.transpose(piece, (0, 1, 3, 2)).reshape(count, W, W)


def unpack_pair(packed, depth_down, depth_up):
    count = 2 ** depth_down
    group = N_COL // count
    width = W // group
    start = pair_start(depth_down, depth_up) * W // N_COL
    piece = packed[:, :, start:start + width].reshape(count, group, W, width)
    return jnp.transpose(piece, (0, 2, 1, 3)).reshape(count, W, W)


def reference(right_side, off_blocks, diag_inverse):
    highest = lax.Precision.HIGHEST
    totals = [jnp.zeros((2 ** depth_now, W, R), jnp.float32) for depth_now in range(LEVELS)]
    forward = [None] * LEVELS
    for depth_now in reversed(range(LEVELS)):
        start_node = 2 ** depth_now - 1
        node_count = 2 ** depth_now
        residue = right_side[start_node:start_node + node_count] - totals[depth_now]
        solved = jnp.einsum("nab,nbr->nar", unpack_diag(diag_inverse, depth_now), residue,
                            precision=highest, preferred_element_type=jnp.float32)
        forward[depth_now] = solved
        for depth_up in range(depth_now):
            groups = 2 ** depth_up
            blocks = unpack_pair(off_blocks, depth_now, depth_up).reshape(groups, node_count // groups, W, W)
            grouped = solved.reshape(groups, node_count // groups, W, R)
            totals[depth_up] = totals[depth_up] + jnp.einsum("gsij,gsjr->gir", blocks, grouped,
                                                             precision=highest, preferred_element_type=jnp.float32)
    totals_down = [jnp.zeros((2 ** depth_now, W, R), jnp.float32) for depth_now in range(LEVELS)]
    backward = [None] * LEVELS
    for depth_now in range(LEVELS):
        node_count = 2 ** depth_now
        residue = forward[depth_now] - totals_down[depth_now]
        solved = jnp.einsum("nba,nbr->nar", unpack_diag(diag_inverse, depth_now), residue,
                            precision=highest, preferred_element_type=jnp.float32)
        backward[depth_now] = solved
        for depth_down in range(depth_now + 1, LEVELS):
            node_down = 2 ** depth_down
            blocks = unpack_pair(off_blocks, depth_down, depth_now).reshape(node_count, node_down // node_count, W, W)
            term = jnp.einsum("gsij,gir->gsjr", blocks, solved,
                              precision=highest, preferred_element_type=jnp.float32)
            totals_down[depth_down] = totals_down[depth_down] + term.reshape(node_down, W, R)
    forward_packed = []
    backward_packed = []
    for depth_now in range(LEVELS):
        group = N_COL // 2 ** depth_now
        forward_packed.append(forward[depth_now].reshape(N_COL, W // group, R))
        backward_packed.append(jnp.repeat(backward[depth_now], group, axis=0))
    return jnp.concatenate(forward_packed, axis=1), jnp.stack(backward_packed, axis=1)
```

```python
import jax
import jax.numpy as jnp
import numpy as np
from jax import lax
from jax.sharding import Mesh, PartitionSpec as P

SIZES = {"z": 8, "x": 4, "y": 4, "core": 2}
PRECISION = lax.Precision.HIGHEST


def shift(value, axis, by):
    size = SIZES[axis]
    return lax.ppermute(value, axis, [(i, (i + by) % size) for i in range(size)])


def swap(value, axis, mask):
    return lax.ppermute(value, axis, [(i, i ^ mask) for i in range(SIZES[axis])])


def ring_z(block):
    half = block.shape[0] // 2
    parts = [block] + [None] * 7
    up = down = block
    for step in range(1, 4):
        up, down = shift(up, "z", 1), shift(down, "z", -1)
        parts[step], parts[8 - step] = up, down
    parts[4] = jnp.concatenate([shift(up[:half], "z", 1), shift(down[half:], "z", -1)], axis=0)
    return parts


def ring_x(block):
    half = block.shape[0] // 2
    up, down = shift(block, "x", 1), shift(block, "x", -1)
    across = jnp.concatenate([shift(up[:half], "x", 1), shift(down[half:], "x", -1)], axis=0)
    return [block, up, across, down]


def mul(matrix, value):
    return lax.dot_general(matrix, value, (((1,), (0,)), ((), ())), precision=PRECISION,
                           preferred_element_type=jnp.float32)


def mul_t(matrix, value):
    return lax.dot_general(matrix, value, (((0,), (0,)), ((), ())), precision=PRECISION,
                           preferred_element_type=jnp.float32)


def cut(array, start, width):
    return lax.slice_in_dim(array, start, start + width, axis=1)


def per_device(right_side, off_blocks, diag_inverse):
    off, diag = off_blocks[0], diag_inverse[0]
    x, y, core = lax.axis_index("x"), lax.axis_index("y"), lax.axis_index("core")
    column = 2 * y + core

    chain = [lax.dynamic_index_in_dim(right_side, 2**k - 1 + (column >> (3 - k)), 0, keepdims=False)
             for k in range(4)]
    stream_a = jnp.concatenate([cut(off, 640, 1536), cut(off, 128, 512)], axis=1)
    rows_a = []
    for k in range(4):
        target = lax.rem(x + k, 4) * 128
        pieces = [lax.dynamic_slice(chain[3], (0, target), (16, 128))]
        pieces += [lax.dynamic_slice(chain[m], (0, target + 64 * core), (16, 64)) for m in (2, 1, 0)]
        block = jnp.concatenate([stream_a] + pieces, axis=1)
        rows_a.append(shift(block, "x", k) if k else block)
    whole_a = jnp.concatenate(ring_z(jnp.concatenate(rows_a, axis=0)), axis=0)

    small = jnp.concatenate([cut(off, 0, 128), cut(diag, 0, 192)], axis=1)
    other = swap(small, "y", 1)
    pair_d0 = jnp.concatenate([cut(small, 128, 64), cut(other, 128, 64)], axis=1)
    stream_b = jnp.concatenate(
        [cut(diag, 448, 512), cut(diag, 192, 256),
         cut(small, 0, 128), cut(other, 0, 128), cut(small, 192, 128), cut(other, 192, 128),
         pair_d0, swap(pair_d0, "y", 2)], axis=1)
    rows_b = ring_x(jnp.stack(ring_z(stream_b), axis=0))
    whole_b = jnp.stack(rows_b, axis=1).reshape(512, 1536)

    l03, l13, l23 = cut(whole_a, 0, 512), cut(whole_a, 512, 512), cut(whole_a, 1024, 512)
    b3, b2, b1, b0 = cut(whole_a, 2048, 128), cut(whole_a, 2176, 64), cut(whole_a, 2240, 64), cut(whole_a, 2304, 64)
    d3 = cut(whole_b, 0, 512)
    mine = jnp.concatenate([cut(whole_a, 1536, 512), cut(whole_b, 512, 1024)], axis=1)
    theirs = swap(mine, "core", 1)

    def both(start):
        return jnp.concatenate([cut(mine, start, 256), cut(theirs, start, 256)], axis=1)

    l02, l12, d2, l01, d1, d0 = (both(256 * i) for i in range(6))

    y3 = mul_t(d3, b3)
    up3 = jnp.concatenate([mul(l23, y3), mul(l13, y3), mul(l03, y3)], axis=0)
    kept = lax.dynamic_slice(up3, (0, 64 * core), (1536, 64))
    given = lax.dynamic_slice(up3, (0, 64 * (1 - core)), (1536, 64))
    up3 = kept + swap(given, "core", 1)
    y2 = mul_t(d2, b2 - up3[:512])
    up2 = up3[512:] + jnp.concatenate([mul(l12, y2), mul(l02, y2)], axis=0)
    up2 = up2 + swap(up2, "y", 1)
    y1 = mul_t(d1, b1 - up2[:512])
    up1 = up2[512:] + mul(l01, y1)
    up1 = up1 + swap(up1, "y", 2)
    y0 = mul_t(d0, b0 - up1)

    own = jnp.concatenate([y0[:64], y1[:128], y2[:256]], axis=0)
    partner = swap(jnp.concatenate([y0[256:320], y1[256:384], y2[256:512]], axis=0), "core", 1)
    low = jnp.where(core == 0, jnp.concatenate([own, partner], axis=1), jnp.concatenate([partner, own], axis=1))
    piece = jnp.concatenate([low, y3], axis=0)
    forward = jnp.zeros((960, 512), jnp.float32)
    for k in range(4):
        part = shift(piece, "x", k) if k else piece
        forward = lax.dynamic_update_slice(forward, part, (0, lax.rem(x + 4 - k, 4) * 128))

    x0 = mul(d0, y0)
    x1 = mul(d1, y1 - mul_t(l01, x0))
    x2 = mul(d2, y2 - mul_t(l02, x0) - mul_t(l12, x1))
    low = jnp.concatenate([x0, x1, x2], axis=0)
    partner = swap(low, "core", 1)
    low = jnp.where(core == 0, jnp.concatenate([low, partner], axis=1), jnp.concatenate([partner, low], axis=1))
    x3 = mul(d3, y3 - mul_t(l03, low[:512]) - mul_t(l13, low[512:1024]) - mul_t(l23, low[1024:]))
    chain_x = jnp.stack([low[:64], low[512:576], low[1024:1088], x3[:64]], axis=0).reshape(4, 4, 16, 128)
    backward = jnp.zeros((4, 16, 512), jnp.float32)
    for k in range(4):
        part = chain_x[:, k]
        part = shift(part, "x", -k) if k else part
        backward = lax.dynamic_update_slice(backward, part, (0, 0, lax.rem(x + k, 4) * 128))
    return forward[None], backward[None]


def solution(mesh):
    split = Mesh(np.asarray(mesh.devices).reshape(8, 4, 4, 2), ("z", "x", "y", "core"))
    row, col = ("z", "x"), ("y", "core")
    return jax.shard_map(
        per_device,
        mesh=split,
        in_specs=(P(None, row, None), P(col, row, None), P(col, row, None)),
        out_specs=(P(col, None, None), P(col, None, row, None)),
        check_vma=False,
    )
```

```python
import functools

import jax
import jax.numpy as jnp
import numpy as np
from jax import lax
from jax.experimental import pallas as pl
from jax.experimental.pallas import tpu as pltpu
from jax.sharding import Mesh, PartitionSpec as P

SIZES = {"z": 8, "x": 4, "y": 4, "core": 2}
F32, BF16 = jnp.float32, jnp.bfloat16


def shift(value, axis, by):
    size = SIZES[axis]
    return lax.ppermute(value, axis, [(i, (i + by) % size) for i in range(size)])


def swap(value, axis, mask):
    return lax.ppermute(value, axis, [(i, i ^ mask) for i in range(SIZES[axis])])


def ring_z(block):
    half = block.shape[0] // 2
    parts = [block] + [None] * 7
    up = down = block
    for step in range(1, 4):
        up, down = shift(up, "z", 1), shift(down, "z", -1)
        parts[step], parts[8 - step] = up, down
    parts[4] = (shift(up[:half], "z", 1), shift(down[half:], "z", -1))
    return parts


def ring_x(block):
    half = block.shape[0] // 2
    up, down = shift(block, "x", 1), shift(block, "x", -1)
    return [block, up, (shift(up[:half], "x", 1), shift(down[half:], "x", -1)), down]


def cut(array, start, width):
    return lax.slice_in_dim(array, start, start + width, axis=1)


def parts_of(value):
    high = value.astype(BF16)
    return high, (value - high.astype(F32)).astype(BF16)


def times(value, high, low, dims):
    vh, vl = parts_of(value)
    dot = functools.partial(lax.dot_general, dimension_numbers=((dims, ((), ()))), preferred_element_type=F32)
    return dot(vh, high) + (dot(vl, high) + dot(vh, low))


def mm(value, matrix):
    return times(value, *matrix, ((1,), (0,)))


def mmt(value, matrix):
    return times(value, *matrix, ((1,), (1,)))


def whole(ref, columns):
    return ref[0, :, columns], ref[1, :, columns]


def rows_of_a(refs):
    order = [(0, 64), (64, 64), (128, 64), (192, 64), (256, 32), (288, 32), (320, 64), (384, 64), (448, 64)]
    return [(start, size, ref) for (start, size), ref in zip(order, refs)]


def rows_of_b(refs):
    found = []
    for k, first, count, ref in ((0, 0, 8, refs[0]), (1, 0, 8, refs[1]), (2, 0, 4, refs[2]), (2, 4, 4, refs[3]),
                                 (3, 0, 8, refs[4])):
        found += [((first + s) * 64 + k * 16, s, ref) for s in range(count)]
    return found


def mine_kernel(*refs):
    out = refs[14]
    for start, size, ref in rows_of_a(refs[:9]):
        out[start:start + size, 0:512] = ref[:, 1536:2048]
    for start, s, ref in rows_of_b(refs[9:14]):
        out[start:start + 16, 512:1536] = ref[s, :, 512:1536]


def level3_kernel(core_ref, *refs):
    a_refs, b_refs = rows_of_a(refs[:9]), rows_of_b(refs[9:14])
    mat, y3_out, y3t_out, kept_out, given_out, b2t_out, b1t_out, b0t_out, rhs, up = refs[14:]
    for start, size, ref in a_refs:
        rhs[start:start + size, 0:320] = ref[:, 2048:2368]
        high, low = parts_of(ref[:, 0:1536])
        mat[0, start:start + size, 0:1536] = high
        mat[1, start:start + size, 0:1536] = low
    for start, s, ref in b_refs:
        high, low = parts_of(ref[s, :, 0:512])
        mat[0, start:start + 16, 1536:2048] = high
        mat[1, start:start + 16, 1536:2048] = low
    rhs[:, 320:384] = jnp.zeros((512, 64), F32)
    b3t = rhs[:, 0:128].T
    b21t = rhs[:, 128:256].T
    b2t_out[...] = b21t[0:64]
    b1t_out[...] = b21t[64:128]
    b0t_out[...] = rhs[:, 256:384].T[0:64]
    y3t = mm(b3t, whole(mat, slice(1536, 2048)))
    y3t_out[...] = y3t
    y3_out[...] = y3t.T
    for at, column in ((0, 1024), (512, 512), (1024, 0)):
        up[:, at:at + 512] = mmt(y3t, whole(mat, slice(column, column + 512)))
    core = core_ref[0]
    kept_out[...] = up[pl.ds(pl.multiple_of(64 * core, 64), 64), :]
    given_out[...] = up[pl.ds(pl.multiple_of(64 * (1 - core), 64), 64), :]


def level2_kernel(mine, theirs, kept, got, b2t, mat, y2t_out, up_out):
    for i in range(6):
        for j, ref in ((0, mine), (256, theirs)):
            high, low = parts_of(ref[:, 256 * i:256 * i + 256])
            mat[0, :, 512 * i + j:512 * i + j + 256] = high
            mat[1, :, 512 * i + j:512 * i + j + 256] = low
    up3 = kept[...] + got[...]
    y2t = mm(b2t[...] - up3[:, 0:512], whole(mat, slice(1024, 1536)))
    y2t_out[...] = y2t
    up_out[:, 0:512] = up3[:, 512:1024] + mmt(y2t, whole(mat, slice(512, 1024)))
    up_out[:, 512:1024] = up3[:, 1024:1536] + mmt(y2t, whole(mat, slice(0, 512)))


def level1_kernel(up_ref, got, b1t, mat, y1t_out, up_out):
    y1t = mm(b1t[...] - (up_ref[:, 0:512] + got[:, 0:512]), whole(mat, slice(2048, 2560)))
    y1t_out[...] = y1t
    up_out[...] = (up_ref[:, 512:1024] + got[:, 512:1024]) + mmt(y1t, whole(mat, slice(1536, 2048)))


def level0_kernel(up_ref, got, b0t, y2t, y1t, mat, y0t_out, low_out):
    l02, l12, d2, l01, d1, d0 = (whole(mat, slice(512 * i, 512 * i + 512)) for i in range(6))
    y0t = mm(b0t[...] - (up_ref[...] + got[...]), d0)
    y0t_out[...] = y0t
    x0t = mmt(y0t, d0)
    low_out[:, 0:512] = x0t
    x1t = mmt(y1t[...] - mm(x0t, l01), d1)
    low_out[:, 512:1024] = x1t
    low_out[:, 1024:1536] = mmt(y2t[...] - mm(x0t, l02) - mm(x1t, l12), d2)


def last_kernel(core_ref, low, got, y3t, mat, x_out, both, tops):
    core = core_ref[0]
    both[pl.ds(pl.multiple_of(64 * core, 64), 64), :] = low[...]
    both[pl.ds(pl.multiple_of(64 * (1 - core), 64), 64), :] = got[...]
    rest = y3t[...]
    for k in range(3):
        rest = rest - mm(both[:, 512 * k:512 * k + 512], whole(mat, slice(512 * k, 512 * k + 512)))
        tops[:, 64 * k:64 * k + 64] = both[:, 512 * k:512 * k + 64]
    tops[:, 192:256] = mmt(rest, (mat[0, 0:64, 1536:2048], mat[1, 0:64, 1536:2048]))
    x_out[...] = tops[...].T


def rows_kernel(core_ref, y0t, y1t, y2t, got, out, both):
    core = core_ref[0]
    here, there = pl.multiple_of(64 * core, 64), pl.multiple_of(64 * (1 - core), 64)
    both[pl.ds(here, 64), 0:64] = y0t[:, 0:64]
    both[pl.ds(here, 64), 64:192] = y1t[:, 0:128]
    both[pl.ds(here, 64), 192:448] = y2t[:, 0:256]
    both[pl.ds(there, 64), 0:448] = got[...]
    both[:, 448:512] = jnp.zeros((128, 64), F32)
    out[...] = both[...].T[0:448]


def call(kernel, name, outs, *args, scalars=0, scratch=()):
    in_specs = [pl.BlockSpec(memory_space=pltpu.SMEM)] * scalars
    in_specs += [pl.BlockSpec(memory_space=pltpu.VMEM)] * (len(args) - scalars)
    return pl.pallas_call(
        kernel,
        name=name,
        out_shape=[jax.ShapeDtypeStruct(shape, kind) for shape, kind in outs],
        in_specs=in_specs,
        out_specs=[pl.BlockSpec(memory_space=pltpu.VMEM)] * len(outs),
        scratch_shapes=list(scratch),
        compiler_params=pltpu.CompilerParams(vmem_limit_bytes=40 * 2**20),
    )(*args)


def per_device(right_side, off_blocks, diag_inverse):
    off, diag = off_blocks[0], diag_inverse[0]
    x, y, core = lax.axis_index("x"), lax.axis_index("y"), lax.axis_index("core")
    column = 2 * y + core
    core_at = jnp.reshape(core, (1,)).astype(jnp.int32)

    chain = [lax.dynamic_index_in_dim(right_side, 2**k - 1 + (column >> (3 - k)), 0, keepdims=False)
             for k in range(4)]
    stream_a = jnp.concatenate([cut(off, 640, 1536), cut(off, 128, 512)], axis=1)
    rows_a = []
    for k in range(4):
        target = lax.rem(x + k, 4) * 128
        pieces = [lax.dynamic_slice(chain[3], (0, target), (16, 128))]
        pieces += [lax.dynamic_slice(chain[m], (0, target + 64 * core), (16, 64)) for m in (2, 1, 0)]
        block = jnp.concatenate([stream_a] + pieces, axis=1)
        rows_a.append(shift(block, "x", k) if k else block)
    blocks_a = ring_z(jnp.concatenate(rows_a, axis=0))
    blocks_a = blocks_a[:4] + list(blocks_a[4]) + blocks_a[5:]

    small = jnp.concatenate([cut(off, 0, 128), cut(diag, 0, 192)], axis=1)
    other = swap(small, "y", 1)
    pair_d0 = jnp.concatenate([cut(small, 128, 64), cut(other, 128, 64)], axis=1)
    stream_b = jnp.concatenate(
        [cut(diag, 448, 512), cut(diag, 192, 256),
         cut(small, 0, 128), cut(other, 0, 128), cut(small, 192, 128), cut(other, 192, 128),
         pair_d0, swap(pair_d0, "y", 2)], axis=1)
    rows_b = ring_z(stream_b)
    rows_b[4] = jnp.concatenate(rows_b[4], axis=0)
    blocks_b = ring_x(jnp.stack(rows_b, axis=0))
    blocks_b = blocks_b[:2] + list(blocks_b[2]) + blocks_b[3:]

    (mine,) = call(mine_kernel, "mine", [((512, 1536), F32)], *blocks_a, *blocks_b)
    theirs = swap(mine, "core", 1)

    mat3, y3, y3t, kept, given, b2t, b1t, b0t = call(
        level3_kernel, "level3",
        [((2, 512, 2048), BF16), ((512, 128), F32), ((128, 512), F32), ((64, 1536), F32), ((64, 1536), F32),
         ((64, 512), F32), ((64, 512), F32), ((64, 512), F32)],
        core_at, *blocks_a, *blocks_b, scalars=1,
        scratch=[pltpu.VMEM((512, 384), F32), pltpu.VMEM((128, 1536), F32)])
    got = swap(given, "core", 1)
    mat, y2t, up = call(level2_kernel, "level2",
                        [((2, 512, 3072), BF16), ((64, 512), F32), ((64, 1024), F32)], mine, theirs, kept, got, b2t)
    got = swap(up, "y", 1)
    y1t, up = call(level1_kernel, "level1", [((64, 512), F32), ((64, 512), F32)], up, got, b1t, mat)
    got = swap(up, "y", 2)
    y0t, low = call(level0_kernel, "level0", [((64, 512), F32), ((64, 1536), F32)], up, got, b0t, y2t, y1t, mat)

    x_all = call(last_kernel, "last", [((256, 128), F32)], core_at, low, swap(low, "core", 1), y3t, mat3, scalars=1,
                 scratch=[pltpu.VMEM((128, 1536), F32), pltpu.VMEM((128, 256), F32)])[0]
    chain_x = x_all.reshape(4, 4, 16, 128)
    backward = jnp.zeros((4, 16, 512), F32)
    for k in range(4):
        part = chain_x[:, k]
        part = shift(part, "x", -k) if k else part
        backward = lax.dynamic_update_slice(backward, part, (0, 0, lax.rem(x + k, 4) * 128))

    got = swap(jnp.concatenate([y0t[:, 256:320], y1t[:, 256:384], y2t[:, 256:512]], axis=1), "core", 1)
    (low_rows,) = call(rows_kernel, "rows", [((448, 128), F32)], core_at, y0t, y1t, y2t, got, scalars=1,
                       scratch=[pltpu.VMEM((128, 512), F32)])
    forward = jnp.zeros((960, 512), F32)
    for first, piece in ((448, y3), (0, low_rows)):
        for k in range(4):
            part = shift(piece, "x", k) if k else piece
            forward = lax.dynamic_update_slice(forward, part, (first, lax.rem(x + 4 - k, 4) * 128))
    return forward[None], backward[None]


def solution(mesh):
    split = Mesh(np.asarray(mesh.devices).reshape(8, 4, 4, 2), ("z", "x", "y", "core"))
    row, col = ("z", "x"), ("y", "core")
    return jax.shard_map(
        per_device,
        mesh=split,
        in_specs=(P(None, row, None), P(col, row, None), P(col, row, None)),
        out_specs=(P(col, None, None), P(col, None, row, None)),
        check_vma=False,
    )
```

```python
import functools

import jax
import jax.numpy as jnp
import numpy as np
from jax import lax
from jax.experimental import pallas as pl
from jax.experimental.pallas import tpu as pltpu
from jax.sharding import Mesh, PartitionSpec as P

SIZES = {"z": 8, "x": 4, "y": 4, "core": 2}
F32, BF16 = jnp.float32, jnp.bfloat16


def shift(value, axis, by):
    size = SIZES[axis]
    return lax.ppermute(value, axis, [(i, (i + by) % size) for i in range(size)])


def swap(value, axis, mask):
    return lax.ppermute(value, axis, [(i, i ^ mask) for i in range(SIZES[axis])])


def ring_z(block, *held):
    half = block.shape[0] // 2
    parts = [block] + [None] * 7
    up = down = block
    for step in range(1, 4):
        if held and step == 3:
            up, down = lax.optimization_barrier((up, down) + held)[:2]
        up, down = shift(up, "z", 1), shift(down, "z", -1)
        parts[step], parts[8 - step] = up, down
    parts[4] = (shift(up[:half], "z", 1), shift(down[half:], "z", -1))
    return parts


def ring_x(block):
    half = block.shape[0] // 2
    up, down = shift(block, "x", 1), shift(block, "x", -1)
    return [block, up, (shift(up[:half], "x", 1), shift(down[half:], "x", -1)), down]


def cut(array, start, width):
    return lax.slice_in_dim(array, start, start + width, axis=1)


def parts_of(value):
    high = value.astype(BF16)
    return high, (value - high.astype(F32)).astype(BF16)


def times(value, high, low, dims):
    count = value.shape[0]
    vh, vl = parts_of(value)
    dot = functools.partial(lax.dot_general, dimension_numbers=((dims, ((), ()))), preferred_element_type=F32)
    main = dot(jnp.concatenate([vh, vl], axis=0), high)
    return main[:count] + (main[count:] + dot(vh, low))


def mm(value, matrix):
    return times(value, *matrix, ((1,), (0,)))


def mmt(value, matrix):
    return times(value, *matrix, ((1,), (1,)))


def whole(ref, columns):
    return ref[0, :, columns], ref[1, :, columns]


def rows_of_a(refs):
    order = [(0, 64), (64, 64), (128, 64), (192, 64), (256, 32), (288, 32), (320, 64), (384, 64), (448, 64)]
    return [(start, size, ref) for (start, size), ref in zip(order, refs)]


def rows_of_b(refs):
    found = []
    for k, first, count, ref in ((0, 0, 8, refs[0]), (1, 0, 8, refs[1]), (2, 0, 4, refs[2]), (2, 4, 4, refs[3]),
                                 (3, 0, 8, refs[4])):
        found += [((first + s) * 64 + k * 16, s, ref) for s in range(count)]
    return found


def put_parts(mat, rows, columns, value):
    high, low = parts_of(value)
    mat[0, rows, columns] = high
    mat[1, rows, columns] = low


def pack_kernel(place, right, off, diag, b_out, *a_outs):
    b_out[:, 1280:1408] = off[:, 0:128]
    b_out[:, 1408:1536] = diag[:, 64:192]
    b_out[:, 1536:1600] = diag[:, 0:64]
    b_out[:, 0:768] = diag[:, 192:960]
    b_out[:, 768:1280] = off[:, 128:640]
    x, core = place[1], place[3]
    column = 2 * place[2] + core
    for k in range(4):
        out = a_outs[k]
        at = pl.ds(pl.multiple_of(lax.rem(x + k, 4) * 128, 128), 128)
        out[:, 0:1536] = off[:, 640:2176]
        out[:, 1536:1664] = right[7 + column, :, at]
        for m in (2, 1, 0):
            both = right[2**m - 1 + lax.shift_right_logical(column, 3 - m), :, at]
            to = 1664 + 64 * (2 - m)
            out[:, to:to + 64] = jnp.where(core == 0, both[:, 0:64], both[:, 64:128])


def column_blocks_kernel(*refs):
    main, low = refs[9], refs[10]
    for at, first, size in zip((0, 1, 2, 3, 4, 4, 5, 6, 7), (0, 0, 0, 0, 0, 8, 0, 0, 0), (16, 16, 16, 16, 8, 8, 16, 16, 16)):
        ref = refs[at + (first > 0) if at <= 4 else at + 1]
        main[at, first:first + size, :] = ref[:, 0:1280]
        low[at, first:first + size, :] = ref[:, 1280:1600]


def low_rows_kernel(b0, b1, b2, b3, out):
    for k, ref in enumerate((b0, b1, b2, b3)):
        for s in range(8):
            at = s * 64 + k * 16
            out[at:at + 16, :] = ref[s, :, 0:128]
            out[512 + at:528 + at, :] = ref[s, :, 128:256]
            out[1024 + at % 256:1040 + at % 256, at // 256 * 64:at // 256 * 64 + 64] = ref[s, :, 256:320]


def pair_kernel(own, other, out):
    for i, ref in enumerate((own, other)):
        out[0:256, 64 * i:64 * i + 64] = ref[1024:1280, 0:64]
        out[256:512, 64 * i:64 * i + 64] = ref[1024:1280, 64:128]


def low_mine_kernel(own, other, pair, far, out):
    out[:, 0:128] = own[0:512]
    out[:, 128:256] = other[0:512]
    out[:, 256:384] = own[512:1024]
    out[:, 384:512] = other[512:1024]
    out[:, 512:640] = pair[...]
    out[:, 640:768] = far[...]


def mine_kernel(*refs):
    out = refs[5]
    for start, s, ref in rows_of_b(refs[:5]):
        out[start:start + 16, 0:256] = ref[s, :, 0:256]
        out[start:start + 16, 256:768] = ref[s, :, 768:1280]


def level3_kernel(place, *refs):
    a_refs, b_refs = rows_of_a(refs[:9]), rows_of_b(refs[9:14])
    mat, keep, y3_out, kept_out, given_out, b2t_out, rhs, up = refs[14:]
    for start, size, ref in a_refs:
        rhs[start:start + size, 0:320] = ref[:, 1536:1856]
        put_parts(mat, slice(start, start + size), slice(0, 1536), ref[:, 0:1536])
    for start, s, ref in b_refs:
        put_parts(mat, slice(start, start + 16), slice(1536, 2048), ref[s, :, 256:768])
    rhs[:, 320:384] = jnp.zeros((512, 64), F32)
    b3t = rhs[:, 0:128].T
    b21t = rhs[:, 128:256].T
    b2t_out[...] = b21t[0:64]
    keep[128:192] = b21t[64:128]
    keep[192:256] = rhs[:, 256:384].T[0:64]
    y3t = mm(b3t, whole(mat, slice(1536, 2048)))
    keep[0:128] = y3t
    y3_out[...] = y3t.T
    for at, column in ((0, 1024), (512, 512), (1024, 0)):
        up[:, at:at + 512] = mmt(y3t, whole(mat, slice(column, column + 512)))
    core = place[3]
    kept_out[...] = up[pl.ds(pl.multiple_of(64 * core, 64), 64), :]
    given_out[...] = up[pl.ds(pl.multiple_of(64 * (1 - core), 64), 64), :]


def level2_kernel(mine, theirs, kept, got, b2t, mat, y2t_out, up_out):

    @pl.loop(0, 8)
    def _(s):
        at = pl.ds(pl.multiple_of(64 * s, 64), 64)
        for i in range(3):
            for j, ref in ((0, mine), (256, theirs)):
                put_parts(mat, at, slice(512 * i + j, 512 * i + j + 256), ref[at, 256 * i:256 * i + 256])

    up3 = kept[...] + got[...]
    y2t = mm(b2t[...] - up3[:, 0:512], whole(mat, slice(0, 512)))
    y2t_out[...] = y2t
    up_out[:, 0:512] = up3[:, 512:1024] + mmt(y2t, whole(mat, slice(1024, 1536)))
    up_out[:, 512:1024] = up3[:, 1024:1536] + mmt(y2t, whole(mat, slice(512, 1024)))


def low_matrices_kernel(mine, theirs, mat):
    @pl.loop(0, 8)
    def _(s):
        at = pl.ds(pl.multiple_of(64 * s, 64), 64)
        for i in range(3):
            for j, ref in ((0, mine), (256, theirs)):
                put_parts(mat, at, slice(512 * i + j, 512 * i + j + 256), ref[at, 256 * i:256 * i + 256])


def level1_kernel(up_ref, got, y2t, mat, keep, y1t_out, up_out, give_out):
    y1t = mm(keep[128:192] - (up_ref[:, 0:512] + got[:, 0:512]), whole(mat, slice(512, 1024)))
    y1t_out[...] = y1t
    up_out[...] = (up_ref[:, 512:1024] + got[:, 512:1024]) + mmt(y1t, whole(mat, slice(0, 512)))
    give_out[:, 0:128] = y1t[:, 256:384]
    give_out[:, 128:384] = y2t[:, 256:512]


def level0_kernel(up_ref, got, y2t, y1t, mat2, mat, keep, y0t_out, low_out):
    d2, l02, l12 = (whole(mat2, slice(512 * i, 512 * i + 512)) for i in range(3))
    l01, d1, d0 = (whole(mat, slice(512 * i, 512 * i + 512)) for i in range(3))
    y0t = mm(keep[192:256] - (up_ref[...] + got[...]), d0)
    y0t_out[...] = y0t
    low_out[:, 1536:1600] = y0t[:, 256:320]
    x0t = mmt(y0t, d0)
    low_out[:, 0:512] = x0t
    x1t = mmt(y1t[...] - mm(x0t, l01), d1)
    low_out[:, 512:1024] = x1t
    low_out[:, 1024:1536] = mmt(y2t[...] - mm(x0t, l02) - mm(x1t, l12), d2)


def halves(place):
    core = place[3]
    return pl.ds(pl.multiple_of(64 * core, 64), 64), pl.ds(pl.multiple_of(64 * (1 - core), 64), 64)


def rows_kernel(place, y1t, y2t, got, out, both):
    here, there = halves(place)
    both[here, 0:128] = y1t[:, 0:128]
    both[here, 128:384] = y2t[:, 0:256]
    both[there, :] = got[...]
    out[...] = both[...].T


def last_kernel(place, low, got, y0t, keep, mat, *refs):
    outs, both, tops = refs[:4], refs[4], refs[5]
    here, there = halves(place)
    both[here, :] = low[:, 0:1536]
    both[there, :] = got[:, 0:1536]
    tops[here, 0:64] = y0t[:, 0:64]
    tops[there, 0:64] = got[:, 1536:1600]
    rest = keep[0:128]
    for k in range(3):
        rest = rest - mm(both[:, 512 * k:512 * k + 512], whole(mat, slice(512 * k, 512 * k + 512)))
        tops[:, 64 * k + 64:64 * k + 128] = both[:, 512 * k:512 * k + 64]
    tops[:, 256:320] = mmt(rest, (mat[0, 0:64, 1536:2048], mat[1, 0:64, 1536:2048]))
    tops[:, 320:384] = jnp.zeros((128, 64), F32)
    rows = tops[...].T
    for k in range(4):
        outs[k][0:64, :] = rows[0:64]
        for n in range(4):
            at = 64 + 64 * n + 16 * ((4 - k) % 4)
            outs[k][64 + 16 * n:80 + 16 * n, :] = rows[at:at + 16]


def forward_kernel(place, *refs):
    out = refs[8]
    for k in range(4):
        at = pl.ds(pl.multiple_of(lax.rem(place[1] + 4 - k, 4) * 128, 128), 128)
        out[0:64, at] = jnp.zeros((64, 128), F32)
        out[64:448, at] = refs[k][...]
        out[448:960, at] = refs[4 + k][...]


def final_kernel(place, m0, m1, m2, m3, forward_in, forward_out, x_out, top, sem):
    del forward_in
    for k, ref in enumerate((m0, m1, m2, m3)):
        at = pl.ds(pl.multiple_of(lax.rem(place[1] + 4 - k, 4) * 128, 128), 128)
        top[:, at] = ref[0:64, :]
        for n in range(4):
            x_out[n, :, at] = ref[64 + 16 * n:80 + 16 * n, :]
    copy = pltpu.make_async_copy(top, forward_out.at[0:64], sem)
    copy.start()
    copy.wait()


VMEM, SMEM, ANY = (pl.BlockSpec(memory_space=m) for m in (pltpu.VMEM, pltpu.SMEM, pl.ANY))


def call(kernel, name, outs, *args, scalars=1, scratch=(), in_specs=None, out_specs=None, aliases=None, limit=6):
    return pl.pallas_call(
        kernel,
        name=name,
        out_shape=[jax.ShapeDtypeStruct(shape, kind) for shape, kind in outs],
        in_specs=in_specs or [SMEM] * scalars + [VMEM] * (len(args) - scalars),
        out_specs=out_specs or [VMEM] * len(outs),
        scratch_shapes=list(scratch),
        input_output_aliases=aliases or {},
        compiler_params=pltpu.CompilerParams(vmem_limit_bytes=limit * 2**20),
    )(*args)


def after(value, *others):
    return lax.optimization_barrier((value,) + others)[0]


def per_device(right_side, off_blocks, diag_inverse):
    place = jnp.stack([lax.axis_index(a) for a in ("z", "x", "y", "core")]).astype(jnp.int32)

    stream_b, *stream_a = call(
        pack_kernel, "pack", [((16, 1600), F32)] + [((16, 1856), F32)] * 4,
        place, right_side, off_blocks[0], diag_inverse[0], limit=8)

    rows_a = [stream_a[0]] + [shift(stream_a[k], "x", k) for k in (1, 2, 3)]
    block_a = jnp.concatenate(rows_a, axis=0)
    blocks_a = ring_z(block_a)
    blocks_a = blocks_a[:4] + list(blocks_a[4]) + blocks_a[5:]

    rows_b = ring_z(stream_b, block_a)
    rows_b = rows_b[:4] + list(rows_b[4]) + rows_b[5:]
    rows_b[0] = after(rows_b[0], blocks_a[1], blocks_a[8])
    main, low_block = call(column_blocks_kernel, "column_blocks", [((8, 16, 1280), F32), ((8, 16, 320), F32)],
                           *rows_b, scalars=0)
    low_blocks = [shift(low_block, "x", k) for k in (1, 2, 3)]
    low_block = after(low_block, blocks_a[2], blocks_a[7])
    (own,) = call(low_rows_kernel, "low_rows", [((1280, 128), F32)], low_block, *low_blocks, scalars=0)
    other = after(swap(own, "y", 1), blocks_a[3], blocks_a[6])
    (pair,) = call(pair_kernel, "pair", [((512, 128), F32)], own, other, scalars=0)
    (low_mine,) = call(low_mine_kernel, "low_mine", [((512, 768), F32)], own, other, pair,
                       after(swap(pair, "y", 2), blocks_a[4], blocks_a[5]), scalars=0)
    low_theirs = swap(low_mine, "core", 1)
    blocks_b = ring_x(main)
    blocks_b = blocks_b[:2] + list(blocks_b[2]) + blocks_b[3:]

    (mine,) = call(mine_kernel, "mine", [((512, 768), F32)], *blocks_b, scalars=0, limit=6)
    theirs = swap(mine, "core", 1)

    mat3, keep, y3, kept, given, b2t = call(
        level3_kernel, "level3",
        [((2, 512, 2048), BF16), ((256, 512), F32), ((512, 128), F32), ((64, 1536), F32), ((64, 1536), F32),
         ((64, 512), F32)],
        place, *blocks_a, *blocks_b,
        scratch=[pltpu.VMEM((512, 384), F32), pltpu.VMEM((128, 1536), F32)])
    got = swap(given, "core", 1)
    mat2, y2t, up = call(
        level2_kernel, "level2", [((2, 512, 1536), BF16), ((64, 512), F32), ((64, 1024), F32)],
        mine, theirs, kept, got, b2t, scalars=0)
    got = swap(up, "y", 1)
    y3 = after(y3, up)
    top_parts = [y3] + [shift(y3, "x", k) for k in (1, 2, 3)]
    (mat1,) = call(low_matrices_kernel, "low_matrices", [((2, 512, 1536), BF16)], low_mine, low_theirs, scalars=0)
    y1t, up, give = call(
        level1_kernel, "level1", [((64, 512), F32), ((64, 512), F32), ((64, 384), F32)],
        up, got, y2t, mat1, keep, scalars=0)
    got = swap(up, "y", 2)
    (rows,) = call(rows_kernel, "rows", [((384, 128), F32)], place, y1t, y2t, swap(give, "core", 1),
                   scratch=[pltpu.VMEM((128, 384), F32)], limit=4)
    got = after(got, rows, *top_parts)
    mid_parts = [rows] + [shift(rows, "x", k) for k in (1, 2, 3)]
    y0t, low = call(level0_kernel, "level0", [((64, 512), F32), ((64, 1600), F32)],
                    up, got, y2t, y1t, mat2, mat1, keep, scalars=0)

    messages = call(last_kernel, "last", [((128, 128), F32)] * 4, place, low, swap(low, "core", 1), y0t, keep, mat3,
                    scratch=[pltpu.VMEM((128, 1536), F32), pltpu.VMEM((128, 384), F32)])
    held = lax.optimization_barrier(tuple(mid_parts + top_parts) + (messages[0],))[:8]
    (forward,) = call(forward_kernel, "forward", [((960, 512), F32)], place, *held, limit=8)
    arrived = [messages[0]] + [shift(after(messages[k], *mid_parts), "x", k) for k in (1, 2, 3)]
    forward, backward = call(
        final_kernel, "final", [((960, 512), F32), ((4, 16, 512), F32)], place, *arrived, forward,
        in_specs=[SMEM] + [VMEM] * 4 + [ANY], out_specs=[ANY, VMEM], aliases={5: 0},
        scratch=[pltpu.VMEM((64, 512), F32), pltpu.SemaphoreType.DMA], limit=4)
    return forward[None], backward[None]


def solution(mesh):
    split = Mesh(np.asarray(mesh.devices).reshape(8, 4, 4, 2), ("z", "x", "y", "core"))
    row, col = ("z", "x"), ("y", "core")
    return jax.shard_map(
        per_device,
        mesh=split,
        in_specs=(P(None, row, None), P(col, row, None), P(col, row, None)),
        out_specs=(P(col, None, None), P(col, None, row, None)),
        check_vma=False,
    )
```

```python
import functools

import jax
import jax.numpy as jnp
import numpy as np
from jax import lax
from jax.experimental import pallas as pl
from jax.experimental.pallas import tpu as pltpu
from jax.sharding import Mesh, PartitionSpec as P

SIZES = {"z": 8, "x": 4, "y": 4, "core": 2}
F32, BF16 = jnp.float32, jnp.bfloat16


def shift(value, axis, by):
    size = SIZES[axis]
    return lax.ppermute(value, axis, [(i, (i + by) % size) for i in range(size)])


def swap(value, axis, mask):
    return lax.ppermute(value, axis, [(i, i ^ mask) for i in range(SIZES[axis])])


def parts_of(value):
    high = value.astype(BF16)
    return high, (value - high.astype(F32)).astype(BF16)


def times(value, high, low, dims):
    count = value.shape[0]
    vh, vl = parts_of(value)
    dot = functools.partial(lax.dot_general, dimension_numbers=((dims, ((), ()))), preferred_element_type=F32)
    main = dot(jnp.concatenate([vh, vl], axis=0), high)
    return main[:count] + (main[count:] + dot(vh, low))


def mm(value, matrix):
    return times(value, *matrix, ((1,), (0,)))


def mmt(value, matrix):
    return times(value, *matrix, ((1,), (1,)))


def whole(ref, columns):
    return ref[0, :, columns], ref[1, :, columns]


def rows_of_a(refs):
    order = [(0, 64), (64, 64), (128, 64), (192, 64), (256, 32), (288, 32), (320, 64), (384, 64), (448, 64)]
    return [(start, size, ref) for (start, size), ref in zip(order, refs)]


def rows_of_b(refs):
    found = []
    for k, first, count, ref in ((0, 0, 8, refs[0]), (1, 0, 8, refs[1]), (2, 0, 4, refs[2]), (2, 4, 4, refs[3]),
                                 (3, 0, 8, refs[4])):
        found += [((first + s) * 64 + k * 16, s, ref) for s in range(count)]
    return found


def put_parts(mat, rows, columns, value):
    high, low = parts_of(value)
    mat[0, rows, columns] = high
    mat[1, rows, columns] = low


def pack_kernel(place, right, off, diag, b_out, *a_outs):
    b_out[:, 1280:1408] = off[:, 0:128]
    b_out[:, 1408:1536] = diag[:, 64:192]
    b_out[:, 1536:1600] = diag[:, 0:64]
    b_out[:, 0:768] = diag[:, 192:960]
    b_out[:, 768:1280] = off[:, 128:640]
    x, core = place[1], place[3]
    column = 2 * place[2] + core
    for k in range(4):
        out = a_outs[k]
        at = pl.ds(pl.multiple_of(lax.rem(x + k, 4) * 128, 128), 128)
        out[:, 0:1536] = off[:, 640:2176]
        out[:, 1536:1664] = right[7 + column, :, at]
        for m in (2, 1, 0):
            both = right[2**m - 1 + lax.shift_right_logical(column, 3 - m), :, at]
            to = 1664 + 64 * (2 - m)
            out[:, to:to + 64] = jnp.where(core == 0, both[:, 0:64], both[:, 64:128])


def column_blocks_kernel(*refs):
    main, low = refs[8], refs[9]
    size = 16
    for first, ref in zip(range(0, 128, 16), refs):
        main[first // 16, :, :] = ref[:, 0:1280]
        low[first:first + size, :] = ref[:, 1280:1408]
        low[128 + first:128 + first + size, :] = ref[:, 1408:1536]
        at = first // 64 * 64
        low[256 + first % 64:256 + first % 64 + size, at:at + 64] = ref[:, 1536:1600]


def pair_kernel(own, other, out):
    for i, ref in enumerate((own, other)):
        out[0:64, 64 * i:64 * i + 64] = ref[256:320, 0:64]
        out[64:128, 64 * i:64 * i + 64] = ref[256:320, 64:128]


def slab_kernel(own, other, pair, far, out):
    out[:, 0:128] = own[0:128]
    out[:, 128:256] = other[0:128]
    out[:, 256:384] = own[128:256]
    out[:, 384:512] = other[128:256]
    out[:, 512:640] = pair[...]
    out[:, 640:768] = far[...]


def low_rows_kernel(b0, b1, b2, b2_low, b3, out):
    for k, refs in enumerate(((b0,), (b1,), (b2, b2_low), (b3,))):
        for s in range(8):
            ref, at = refs[s // 4 if len(refs) > 1 else 0], 16 * (s % 4 if len(refs) > 1 else s)
            out[s * 64 + k * 16:s * 64 + k * 16 + 16, :] = ref[at:at + 16, :]


def mine_kernel(*refs):
    out = refs[5]
    for start, s, ref in rows_of_b(refs[:5]):
        out[start:start + 16, 0:256] = ref[s, :, 0:256]
        out[start:start + 16, 256:768] = ref[s, :, 768:1280]


def level3_kernel(place, *refs):
    a_refs, b_refs = rows_of_a(refs[:9]), rows_of_b(refs[9:14])
    mat, keep, y3_out, kept_out, given_out, b2t_out, rhs, up = refs[14:]
    for start, size, ref in a_refs:
        rhs[start:start + size, 0:320] = ref[:, 1536:1856]
        put_parts(mat, slice(start, start + size), slice(0, 1536), ref[:, 0:1536])
    for start, s, ref in b_refs:
        put_parts(mat, slice(start, start + 16), slice(1536, 2048), ref[s, :, 256:768])
    rhs[:, 320:384] = jnp.zeros((512, 64), F32)
    b3t = rhs[:, 0:128].T
    b21t = rhs[:, 128:256].T
    b2t_out[...] = b21t[0:64]
    keep[128:192] = b21t[64:128]
    keep[192:256] = rhs[:, 256:384].T[0:64]
    y3t = mm(b3t, whole(mat, slice(1536, 2048)))
    keep[0:128] = y3t
    y3_out[...] = y3t.T
    for at, column in ((0, 1024), (512, 512), (1024, 0)):
        up[:, at:at + 512] = mmt(y3t, whole(mat, slice(column, column + 512)))
    core = place[3]
    kept_out[...] = up[pl.ds(pl.multiple_of(64 * core, 64), 64), :]
    given_out[...] = up[pl.ds(pl.multiple_of(64 * (1 - core), 64), 64), :]


def level2_kernel(mine, theirs, kept, got, b2t, mat, y2t_out, up_out):

    @pl.loop(0, 8)
    def _(s):
        at = pl.ds(pl.multiple_of(64 * s, 64), 64)
        for i in range(3):
            for j, ref in ((0, mine), (256, theirs)):
                put_parts(mat, at, slice(512 * i + j, 512 * i + j + 256), ref[at, 256 * i:256 * i + 256])

    up3 = kept[...] + got[...]
    y2t = mm(b2t[...] - up3[:, 0:512], whole(mat, slice(0, 512)))
    y2t_out[...] = y2t
    up_out[:, 0:512] = up3[:, 512:1024] + mmt(y2t, whole(mat, slice(1024, 1536)))
    up_out[:, 512:1024] = up3[:, 1024:1536] + mmt(y2t, whole(mat, slice(512, 1024)))


def low_matrices_kernel(mine, theirs, mat):
    @pl.loop(0, 8)
    def _(s):
        at = pl.ds(pl.multiple_of(64 * s, 64), 64)
        for i in range(3):
            for j, ref in ((0, mine), (256, theirs)):
                put_parts(mat, at, slice(512 * i + j, 512 * i + j + 256), ref[at, 256 * i:256 * i + 256])


def level1_kernel(up_ref, got, y2t, mat, keep, y1t_out, up_out, give_out):
    y1t = mm(keep[128:192] - (up_ref[:, 0:512] + got[:, 0:512]), whole(mat, slice(512, 1024)))
    y1t_out[...] = y1t
    up_out[...] = (up_ref[:, 512:1024] + got[:, 512:1024]) + mmt(y1t, whole(mat, slice(0, 512)))
    give_out[:, 0:128] = y1t[:, 256:384]
    give_out[:, 128:384] = y2t[:, 256:512]


def level0_kernel(up_ref, got, y2t, y1t, mat2, mat, keep, y0t_out, low_out):
    d2, l02, l12 = (whole(mat2, slice(512 * i, 512 * i + 512)) for i in range(3))
    l01, d1, d0 = (whole(mat, slice(512 * i, 512 * i + 512)) for i in range(3))
    y0t = mm(keep[192:256] - (up_ref[...] + got[...]), d0)
    y0t_out[...] = y0t
    low_out[:, 1536:1600] = y0t[:, 256:320]
    x0t = mmt(y0t, d0)
    low_out[:, 0:512] = x0t
    x1t = mmt(y1t[...] - mm(x0t, l01), d1)
    low_out[:, 512:1024] = x1t
    low_out[:, 1024:1536] = mmt(y2t[...] - mm(x0t, l02) - mm(x1t, l12), d2)


def halves(place):
    core = place[3]
    return pl.ds(pl.multiple_of(64 * core, 64), 64), pl.ds(pl.multiple_of(64 * (1 - core), 64), 64)


def rows_kernel(place, y1t, y2t, got, out, both):
    here, there = halves(place)
    both[here, 0:128] = y1t[:, 0:128]
    both[here, 128:384] = y2t[:, 0:256]
    both[there, :] = got[...]
    out[...] = both[...].T


def last_kernel(place, low, got, y0t, keep, mat, *refs):
    outs, both, tops = refs[:4], refs[4], refs[5]
    here, there = halves(place)
    both[here, :] = low[:, 0:1536]
    both[there, :] = got[:, 0:1536]
    tops[here, 0:64] = y0t[:, 0:64]
    tops[there, 0:64] = got[:, 1536:1600]
    rest = keep[0:128]
    for k in range(3):
        rest = rest - mm(both[:, 512 * k:512 * k + 512], whole(mat, slice(512 * k, 512 * k + 512)))
        tops[:, 64 * k + 64:64 * k + 128] = both[:, 512 * k:512 * k + 64]
    tops[:, 256:320] = mmt(rest, (mat[0, 0:64, 1536:2048], mat[1, 0:64, 1536:2048]))
    tops[:, 320:384] = jnp.zeros((128, 64), F32)
    rows = tops[...].T
    for k in range(4):
        outs[k][0:64, :] = rows[0:64]
        for n in range(4):
            at = 64 + 64 * n + 16 * ((4 - k) % 4)
            outs[k][64 + 16 * n:80 + 16 * n, :] = rows[at:at + 16]


def forward_kernel(place, *refs):
    out = refs[8]
    for k in range(4):
        at = pl.ds(pl.multiple_of(lax.rem(place[1] + 4 - k, 4) * 128, 128), 128)
        out[0:64, at] = jnp.zeros((64, 128), F32)
        out[64:448, at] = refs[k][...]
        out[448:960, at] = refs[4 + k][...]


def final_kernel(place, m0, m1, m2, m3, forward_in, forward_out, x_out, top, sem):
    del forward_in
    for k, ref in enumerate((m0, m1, m2, m3)):
        at = pl.ds(pl.multiple_of(lax.rem(place[1] + 4 - k, 4) * 128, 128), 128)
        top[:, at] = ref[0:64, :]
        for n in range(4):
            x_out[n, :, at] = ref[64 + 16 * n:80 + 16 * n, :]
    copy = pltpu.make_async_copy(top, forward_out.at[0:64], sem)
    copy.start()
    copy.wait()


VMEM, SMEM, ANY = (pl.BlockSpec(memory_space=m) for m in (pltpu.VMEM, pltpu.SMEM, pl.ANY))


def call(kernel, name, outs, *args, scalars=1, scratch=(), in_specs=None, out_specs=None, aliases=None, limit=6):
    return pl.pallas_call(
        kernel,
        name=name,
        out_shape=[jax.ShapeDtypeStruct(shape, kind) for shape, kind in outs],
        in_specs=in_specs or [SMEM] * scalars + [VMEM] * (len(args) - scalars),
        out_specs=out_specs or [VMEM] * len(outs),
        scratch_shapes=list(scratch),
        input_output_aliases=aliases or {},
        compiler_params=pltpu.CompilerParams(vmem_limit_bytes=limit * 2**20),
    )(*args)


def after(value, *others):
    return lax.optimization_barrier((value,) + others)[0]


def per_device(right_side, off_blocks, diag_inverse):
    place = jnp.stack([lax.axis_index(a) for a in ("z", "x", "y", "core")]).astype(jnp.int32)

    stream_b, *stream_a = call(
        pack_kernel, "pack", [((16, 1600), F32)] + [((16, 1856), F32)] * 4,
        place, right_side, off_blocks[0], diag_inverse[0], limit=8)

    wait = lax.optimization_barrier

    def both_ways(up, down, axis):
        return shift(up, axis, 1), shift(down, axis, -1)

    b1 = both_ways(stream_b, stream_b, "z")
    *b1, a_1, a_2, a_3 = wait((*b1, *stream_a[1:]))
    b2 = both_ways(*b1, "z")
    across = [shift(a_1, "x", 1), shift(a_2, "x", 2), shift(a_3, "x", 3)]
    b3 = both_ways(*b2, "z")
    b4 = shift(b3[0], "z", 1)
    b4, *b3, across1, across2, across3 = wait((b4, *b3, *across))
    block_a = jnp.concatenate([stream_a[0], across1, across2, across3], axis=0)
    a1 = both_ways(block_a, block_a, "z")
    main, low = call(column_blocks_kernel, "column_blocks", [((8, 16, 1280), F32), ((320, 128), F32)],
                     stream_b, b1[0], b2[0], b3[0], b4, b3[1], b2[1], b1[1], scalars=0)
    c1_up, c1_down = both_ways(main, main, "x")
    other = swap(low, "y", 1)
    other, a1_up, a1_down = wait((other, *a1))
    a2 = both_ways(a1_up, a1_down, "z")
    (pair,) = call(pair_kernel, "pair", [((128, 128), F32)], low, other, scalars=0)
    far = swap(pair, "y", 2)
    c2 = both_ways(c1_up[:4], c1_down[4:], "x")
    a2_up, a2_down, far = wait((*a2, far))
    a3 = both_ways(a2_up, a2_down, "z")
    (slab,) = call(slab_kernel, "slab", [((128, 768), F32)], low, other, pair, far, scalars=0)
    e1 = both_ways(slab, slab, "x")
    a3_up, a3_down, c2_up, c2_down, e1_up, e1_down = wait((*a3, *c2, *e1))
    a4 = both_ways(a3_up[:32], a3_down[32:], "z")
    e2 = both_ways(e1_up[:64], e1_down[64:], "x")
    *a4, e2_up, e2_down = wait((*a4, *e2))
    blocks_b = [main, c1_up, c2_up, c2_down, c1_down]
    blocks_a = [block_a, a1_up, a2_up, a3_up, a4[0], a4[1], a3_down, a2_down, a1_down]

    (mine,) = call(mine_kernel, "mine", [((512, 768), F32)], *blocks_b, scalars=0, limit=6)
    theirs = swap(mine, "core", 1)

    mat3, keep, y3, kept, given, b2t = call(
        level3_kernel, "level3",
        [((2, 512, 2048), BF16), ((256, 512), F32), ((512, 128), F32), ((64, 1536), F32), ((64, 1536), F32),
         ((64, 512), F32)],
        place, *blocks_a, *blocks_b,
        scratch=[pltpu.VMEM((512, 384), F32), pltpu.VMEM((128, 1536), F32)])
    got = swap(given, "core", 1)
    slab, _ = wait((slab, given))
    (low_mine,) = call(low_rows_kernel, "low_rows", [((512, 768), F32)], slab, e1_up, e2_up, e2_down, e1_down, scalars=0)
    mat2, y2t, up = call(
        level2_kernel, "level2", [((2, 512, 1536), BF16), ((64, 512), F32), ((64, 1024), F32)],
        mine, theirs, kept, got, b2t, scalars=0)
    got = swap(up, "y", 1)
    low_theirs = swap(wait((low_mine, up))[0], "core", 1)
    y3 = after(y3, up)
    top_parts = [y3] + [shift(y3, "x", k) for k in (1, 2, 3)]
    (mat1,) = call(low_matrices_kernel, "low_matrices", [((2, 512, 1536), BF16)], low_mine, low_theirs, scalars=0)
    y1t, up, give = call(
        level1_kernel, "level1", [((64, 512), F32), ((64, 512), F32), ((64, 384), F32)],
        up, got, y2t, mat1, keep, scalars=0)
    got = swap(up, "y", 2)
    (rows,) = call(rows_kernel, "rows", [((384, 128), F32)], place, y1t, y2t, swap(give, "core", 1),
                   scratch=[pltpu.VMEM((128, 384), F32)], limit=4)
    got = after(got, rows, *top_parts)
    mid_parts = [rows] + [shift(rows, "x", k) for k in (1, 2, 3)]
    y0t, low = call(level0_kernel, "level0", [((64, 512), F32), ((64, 1600), F32)],
                    up, got, y2t, y1t, mat2, mat1, keep, scalars=0)

    messages = call(last_kernel, "last", [((128, 128), F32)] * 4, place, low, swap(low, "core", 1), y0t, keep, mat3,
                    scratch=[pltpu.VMEM((128, 1536), F32), pltpu.VMEM((128, 384), F32)])
    held = lax.optimization_barrier(tuple(mid_parts + top_parts) + (messages[0],))[:8]
    (forward,) = call(forward_kernel, "forward", [((960, 512), F32)], place, *held, limit=8)
    arrived = [messages[0]] + [shift(messages[k], "x", k) for k in (1, 2, 3)]
    forward, backward = call(
        final_kernel, "final", [((960, 512), F32), ((4, 16, 512), F32)], place, *arrived, forward,
        in_specs=[SMEM] + [VMEM] * 4 + [ANY], out_specs=[ANY, VMEM], aliases={5: 0},
        scratch=[pltpu.VMEM((64, 512), F32), pltpu.SemaphoreType.DMA], limit=4)
    return forward[None], backward[None]


def solution(mesh):
    split = Mesh(np.asarray(mesh.devices).reshape(8, 4, 4, 2), ("z", "x", "y", "core"))
    row, col = ("z", "x"), ("y", "core")
    return jax.shard_map(
        per_device,
        mesh=split,
        in_specs=(P(None, row, None), P(col, row, None), P(col, row, None)),
        out_specs=(P(col, None, None), P(col, None, row, None)),
        check_vma=False,
    )
```

```python
import functools

import jax
import jax.numpy as jnp
import numpy as np
from jax import lax
from jax.experimental import pallas as pl
from jax.experimental.pallas import tpu as pltpu
from jax.sharding import Mesh, PartitionSpec as P

SIZES = {"z": 8, "x": 4, "y": 4, "core": 2}
F32, BF16 = jnp.float32, jnp.bfloat16


def shift(value, axis, by):
    size = SIZES[axis]
    return lax.ppermute(value, axis, [(i, (i + by) % size) for i in range(size)])


def swap(value, axis, mask):
    return lax.ppermute(value, axis, [(i, i ^ mask) for i in range(SIZES[axis])])


def parts_of(value):
    high = value.astype(BF16)
    return high, (value - high.astype(F32)).astype(BF16)


def times(value, high, low, dims):
    count = value.shape[0]
    vh, vl = parts_of(value)
    dot = functools.partial(lax.dot_general, dimension_numbers=((dims, ((), ()))), preferred_element_type=F32)
    main = dot(jnp.concatenate([vh, vl], axis=0), high)
    return main[:count] + (main[count:] + dot(vh, low))


def mm(value, matrix):
    return times(value, *matrix, ((1,), (0,)))


def mmt(value, matrix):
    return times(value, *matrix, ((1,), (1,)))


def whole(ref, columns):
    return ref[0, :, columns], ref[1, :, columns]


def rows_of_a(refs):
    order = [(0, 64), (64, 64), (128, 64), (192, 64), (256, 32), (288, 32), (320, 64), (384, 64), (448, 64)]
    return [(start, size, ref) for (start, size), ref in zip(order, refs)]


def rows_of_b(refs):
    found = []
    for k, first, count, ref in ((0, 0, 8, refs[0]), (1, 0, 8, refs[1]), (2, 0, 4, refs[2]), (2, 4, 4, refs[3]),
                                 (3, 0, 8, refs[4])):
        found += [((first + s) * 64 + k * 16, s, ref) for s in range(count)]
    return found


def put_parts(mat, rows, columns, value):
    high, low = parts_of(value)
    mat[0, rows, columns] = high
    mat[1, rows, columns] = low


def pack_kernel(place, right, off, diag, b_out, *a_outs):
    b_out[:, 1280:1408] = off[:, 0:128]
    b_out[:, 1408:1536] = diag[:, 64:192]
    b_out[:, 1536:1600] = diag[:, 0:64]
    b_out[:, 0:768] = diag[:, 192:960]
    b_out[:, 768:1280] = off[:, 128:640]
    x, core = place[1], place[3]
    column = 2 * place[2] + core
    for k in range(4):
        out = a_outs[k]
        at = pl.ds(pl.multiple_of(lax.rem(x + k, 4) * 128, 128), 128)
        out[:, 0:1536] = off[:, 640:2176]
        out[:, 1536:1664] = right[7 + column, :, at]
        for m in (2, 1, 0):
            both = right[2**m - 1 + lax.shift_right_logical(column, 3 - m), :, at]
            to = 1664 + 64 * (2 - m)
            out[:, to:to + 64] = jnp.where(core == 0, both[:, 0:64], both[:, 64:128])


def column_blocks_kernel(*refs):
    main, low = refs[8], refs[9]
    size = 16
    for first, ref in zip(range(0, 128, 16), refs):
        main[first // 16, :, :] = ref[:, 0:1280]
        low[first:first + size, :] = ref[:, 1280:1408]
        low[128 + first:128 + first + size, :] = ref[:, 1408:1536]
        at = first // 64 * 64
        low[256 + first % 64:256 + first % 64 + size, at:at + 64] = ref[:, 1536:1600]


def pair_kernel(own, other, out):
    for i, ref in enumerate((own, other)):
        out[0:64, 64 * i:64 * i + 64] = ref[256:320, 0:64]
        out[64:128, 64 * i:64 * i + 64] = ref[256:320, 64:128]


def slab_kernel(own, other, pair, far, out):
    out[:, 0:128] = own[0:128]
    out[:, 128:256] = other[0:128]
    out[:, 256:384] = own[128:256]
    out[:, 384:512] = other[128:256]
    out[:, 512:640] = pair[...]
    out[:, 640:768] = far[...]


def low_rows_kernel(b0, b1, b2, b2_low, b3, out):
    for k, refs in enumerate(((b0,), (b1,), (b2, b2_low), (b3,))):
        for s in range(8):
            ref, at = refs[s // 4 if len(refs) > 1 else 0], 16 * (s % 4 if len(refs) > 1 else s)
            out[s * 64 + k * 16:s * 64 + k * 16 + 16, :] = ref[at:at + 16, :]


def mine_kernel(*refs):
    out = refs[5]
    for start, s, ref in rows_of_b(refs[:5]):
        out[start:start + 16, 0:256] = ref[s, :, 0:256]
        out[start:start + 16, 256:768] = ref[s, :, 768:1280]


def level3_kernel(place, *refs):
    a_refs, b_refs = rows_of_a(refs[:9]), rows_of_b(refs[9:14])
    mat, keep, y3_out, kept_out, given_out, b2t_out, rhs, up = refs[14:]
    for start, size, ref in a_refs:
        rhs[start:start + size, 0:320] = ref[:, 1536:1856]
        put_parts(mat, slice(start, start + size), slice(0, 1536), ref[:, 0:1536])
    for start, s, ref in b_refs:
        put_parts(mat, slice(start, start + 16), slice(1536, 2048), ref[s, :, 256:768])
    rhs[:, 320:384] = jnp.zeros((512, 64), F32)
    b3t = rhs[:, 0:128].T
    b21t = rhs[:, 128:256].T
    b2t_out[...] = b21t[0:64]
    keep[128:192] = b21t[64:128]
    keep[192:256] = rhs[:, 256:384].T[0:64]
    y3t = mm(b3t, whole(mat, slice(1536, 2048)))
    keep[0:128] = y3t
    y3_out[...] = y3t.T
    for at, column in ((0, 1024), (512, 512), (1024, 0)):
        up[:, at:at + 512] = mmt(y3t, whole(mat, slice(column, column + 512)))
    core = place[3]
    kept_out[...] = up[pl.ds(pl.multiple_of(64 * core, 64), 64), :]
    given_out[...] = up[pl.ds(pl.multiple_of(64 * (1 - core), 64), 64), :]


def level2_kernel(mine, theirs, kept, got, b2t, mat, y2t_out, up_out):

    @pl.loop(0, 8)
    def _(s):
        at = pl.ds(pl.multiple_of(64 * s, 64), 64)
        for i in range(3):
            for j, ref in ((0, mine), (256, theirs)):
                put_parts(mat, at, slice(512 * i + j, 512 * i + j + 256), ref[at, 256 * i:256 * i + 256])

    up3 = kept[...] + got[...]
    y2t = mm(b2t[...] - up3[:, 0:512], whole(mat, slice(0, 512)))
    y2t_out[...] = y2t
    up_out[:, 0:512] = up3[:, 512:1024] + mmt(y2t, whole(mat, slice(1024, 1536)))
    up_out[:, 512:1024] = up3[:, 1024:1536] + mmt(y2t, whole(mat, slice(512, 1024)))


def low_matrices_kernel(mine, theirs, mat):
    @pl.loop(0, 8)
    def _(s):
        at = pl.ds(pl.multiple_of(64 * s, 64), 64)
        for i in range(3):
            for j, ref in ((0, mine), (256, theirs)):
                put_parts(mat, at, slice(512 * i + j, 512 * i + j + 256), ref[at, 256 * i:256 * i + 256])


def level1_kernel(up_ref, got, y2t, mat, keep, y1t_out, up_out, give_out):
    y1t = mm(keep[128:192] - (up_ref[:, 0:512] + got[:, 0:512]), whole(mat, slice(512, 1024)))
    y1t_out[...] = y1t
    up_out[...] = (up_ref[:, 512:1024] + got[:, 512:1024]) + mmt(y1t, whole(mat, slice(0, 512)))
    give_out[:, 0:128] = y1t[:, 256:384]
    give_out[:, 128:384] = y2t[:, 256:512]


def level0_kernel(up_ref, got, y2t, y1t, mat2, mat, keep, y0t_out, low_out):
    d2, l02, l12 = (whole(mat2, slice(512 * i, 512 * i + 512)) for i in range(3))
    l01, d1, d0 = (whole(mat, slice(512 * i, 512 * i + 512)) for i in range(3))
    y0t = mm(keep[192:256] - (up_ref[...] + got[...]), d0)
    y0t_out[...] = y0t
    low_out[:, 1536:1600] = y0t[:, 256:320]
    x0t = mmt(y0t, d0)
    low_out[:, 0:512] = x0t
    x1t = mmt(y1t[...] - mm(x0t, l01), d1)
    low_out[:, 512:1024] = x1t
    low_out[:, 1024:1536] = mmt(y2t[...] - mm(x0t, l02) - mm(x1t, l12), d2)


def halves(place):
    core = place[3]
    return pl.ds(pl.multiple_of(64 * core, 64), 64), pl.ds(pl.multiple_of(64 * (1 - core), 64), 64)


def rows_kernel(place, y1t, y2t, got, out, both):
    here, there = halves(place)
    both[here, 0:128] = y1t[:, 0:128]
    both[here, 128:384] = y2t[:, 0:256]
    both[there, :] = got[...]
    out[...] = both[...].T


def last_kernel(place, low, got, y0t, keep, mat, *refs):
    outs, both, tops = refs[:4], refs[4], refs[5]
    here, there = halves(place)
    both[here, :] = low[:, 0:1536]
    both[there, :] = got[:, 0:1536]
    tops[here, 0:64] = y0t[:, 0:64]
    tops[there, 0:64] = got[:, 1536:1600]
    rest = keep[0:128]
    for k in range(3):
        rest = rest - mm(both[:, 512 * k:512 * k + 512], whole(mat, slice(512 * k, 512 * k + 512)))
        tops[:, 64 * k + 64:64 * k + 128] = both[:, 512 * k:512 * k + 64]
    tops[:, 256:320] = mmt(rest, (mat[0, 0:64, 1536:2048], mat[1, 0:64, 1536:2048]))
    tops[:, 320:384] = jnp.zeros((128, 64), F32)
    rows = tops[...].T
    for k in range(4):
        outs[k][0:64, :] = rows[0:64]
        for n in range(4):
            at = 64 + 64 * n + 16 * ((4 - k) % 4)
            outs[k][64 + 16 * n:80 + 16 * n, :] = rows[at:at + 16]


def forward_kernel(place, p0, p1, p2, p3, out):
    for k, ref in enumerate((p0, p1, p2, p3)):
        at = pl.ds(pl.multiple_of(lax.rem(place[1] + 4 - k, 4) * 128, 128), 128)
        out[0:448, at] = jnp.zeros((448, 128), F32)
        out[448:960, at] = ref[...]


def final_kernel(place, m0, m1, m2, m3, r0, r1, r2, r3, forward_in, forward_out, x_hbm, top, x_out, sems):
    del forward_in
    for k, (ref, rows) in enumerate(((m0, r0), (m1, r1), (m2, r2), (m3, r3))):
        at = pl.ds(pl.multiple_of(lax.rem(place[1] + 4 - k, 4) * 128, 128), 128)
        top[0:64, at] = ref[0:64, :]
        top[64:448, at] = rows[...]
        for n in range(4):
            x_out[n, :, at] = ref[64 + 16 * n:80 + 16 * n, :]
    copies = (pltpu.make_async_copy(top, forward_out.at[0:448], sems.at[0]), pltpu.make_async_copy(x_out, x_hbm, sems.at[1]))
    for copy in copies:
        copy.start()
    for copy in copies:
        copy.wait()


VMEM, SMEM, ANY = (pl.BlockSpec(memory_space=m) for m in (pltpu.VMEM, pltpu.SMEM, pl.ANY))


def call(kernel, name, outs, *args, scalars=1, scratch=(), in_specs=None, out_specs=None, aliases=None, limit=6):
    return pl.pallas_call(
        kernel,
        name=name,
        out_shape=[jax.ShapeDtypeStruct(shape, kind) for shape, kind in outs],
        in_specs=in_specs or [SMEM] * scalars + [VMEM] * (len(args) - scalars),
        out_specs=out_specs or [VMEM] * len(outs),
        scratch_shapes=list(scratch),
        input_output_aliases=aliases or {},
        compiler_params=pltpu.CompilerParams(vmem_limit_bytes=limit * 2**20),
    )(*args)


def after(value, *others):
    return lax.optimization_barrier((value,) + others)[0]


def per_device(right_side, off_blocks, diag_inverse):
    place = jnp.stack([lax.axis_index(a) for a in ("z", "x", "y", "core")]).astype(jnp.int32)

    stream_b, *stream_a = call(
        pack_kernel, "pack", [((16, 1600), F32)] + [((16, 1856), F32)] * 4,
        place, right_side, off_blocks[0], diag_inverse[0], limit=8)

    wait = lax.optimization_barrier

    def both_ways(up, down, axis):
        return shift(up, axis, 1), shift(down, axis, -1)

    b1 = both_ways(stream_b, stream_b, "z")
    *b1, a_1, a_2, a_3, far_b = wait((*b1, *stream_a[1:], stream_b))
    b2 = both_ways(*b1, "z")
    b4 = shift(far_b, "z", 4)
    across = [shift(a_1, "x", 1), shift(a_2, "x", 2), shift(a_3, "x", 3)]
    b3 = both_ways(*b2, "z")
    b4, *b3, across1, across2, across3 = wait((b4, *b3, *across))
    block_a = jnp.concatenate([stream_a[0], across1, across2, across3], axis=0)
    a1 = both_ways(block_a, block_a, "z")
    main, low = call(column_blocks_kernel, "column_blocks", [((8, 16, 1280), F32), ((320, 128), F32)],
                     stream_b, b1[0], b2[0], b3[0], b4, b3[1], b2[1], b1[1], scalars=0)
    c1_up, c1_down = both_ways(main, main, "x")
    other = swap(low, "y", 1)
    other, a1_up, a1_down = wait((other, *a1))
    a2 = both_ways(a1_up, a1_down, "z")
    (pair,) = call(pair_kernel, "pair", [((128, 128), F32)], low, other, scalars=0)
    far = swap(pair, "y", 2)
    c2 = both_ways(c1_up[:4], c1_down[4:], "x")
    a2_up, a2_down, far = wait((*a2, far))
    a3 = both_ways(a2_up, a2_down, "z")
    (slab,) = call(slab_kernel, "slab", [((128, 768), F32)], low, other, pair, far, scalars=0)
    e1 = both_ways(slab, slab, "x")
    a3_up, a3_down, c2_up, c2_down, e1_up, e1_down = wait((*a3, *c2, *e1))
    a4 = both_ways(a3_up[:32], a3_down[32:], "z")
    e2 = both_ways(e1_up[:64], e1_down[64:], "x")
    *a4, e2_up, e2_down = wait((*a4, *e2))
    blocks_b = [main, c1_up, c2_up, c2_down, c1_down]
    blocks_a = [block_a, a1_up, a2_up, a3_up, a4[0], a4[1], a3_down, a2_down, a1_down]

    (mine,) = call(mine_kernel, "mine", [((512, 768), F32)], *blocks_b, scalars=0, limit=6)
    theirs = swap(mine, "core", 1)

    mat3, keep, y3, kept, given, b2t = call(
        level3_kernel, "level3",
        [((2, 512, 2048), BF16), ((256, 512), F32), ((512, 128), F32), ((64, 1536), F32), ((64, 1536), F32),
         ((64, 512), F32)],
        place, *blocks_a, *blocks_b,
        scratch=[pltpu.VMEM((512, 384), F32), pltpu.VMEM((128, 1536), F32)])
    got = swap(given, "core", 1)
    slab, _ = wait((slab, given))
    (low_mine,) = call(low_rows_kernel, "low_rows", [((512, 768), F32)], slab, e1_up, e2_up, e2_down, e1_down, scalars=0)
    mat2, y2t, up = call(
        level2_kernel, "level2", [((2, 512, 1536), BF16), ((64, 512), F32), ((64, 1024), F32)],
        mine, theirs, kept, got, b2t, scalars=0)
    got = swap(up, "y", 1)
    low_theirs = swap(wait((low_mine, up))[0], "core", 1)
    y3 = after(y3, up)
    top_parts = [y3] + [shift(y3, "x", k) for k in (1, 2, 3)]
    (mat1,) = call(low_matrices_kernel, "low_matrices", [((2, 512, 1536), BF16)], low_mine, low_theirs, scalars=0)
    y1t, up, give = call(
        level1_kernel, "level1", [((64, 512), F32), ((64, 512), F32), ((64, 384), F32)],
        up, got, y2t, mat1, keep, scalars=0)
    got = swap(up, "y", 2)
    (rows,) = call(rows_kernel, "rows", [((384, 128), F32)], place, y1t, y2t, swap(give, "core", 1),
                   scratch=[pltpu.VMEM((128, 384), F32)], limit=4)
    got = after(got, rows, *top_parts)
    mid_parts = [rows] + [shift(rows, "x", k) for k in (1, 2, 3)]
    y0t, low = call(level0_kernel, "level0", [((64, 512), F32), ((64, 1600), F32)],
                    up, got, y2t, y1t, mat2, mat1, keep, scalars=0)

    messages = call(last_kernel, "last", [((128, 128), F32)] * 4, place, low, swap(low, "core", 1), y0t, keep, mat3,
                    scratch=[pltpu.VMEM((128, 1536), F32), pltpu.VMEM((128, 384), F32)])
    held = wait(tuple(top_parts) + (messages[0],))[:4]
    (forward,) = call(forward_kernel, "forward", [((960, 512), F32)], place, *held, limit=8)
    arrived = [messages[0]] + [shift(messages[k], "x", k) for k in (1, 2, 3)]
    forward, backward = call(
        final_kernel, "final", [((960, 512), F32), ((4, 16, 512), F32)],
        place, *arrived, *mid_parts, forward,
        in_specs=[SMEM] + [VMEM] * 8 + [ANY], out_specs=[ANY, ANY], aliases={9: 0},
        scratch=[pltpu.VMEM((448, 512), F32), pltpu.VMEM((4, 16, 512), F32), pltpu.SemaphoreType.DMA((2,))], limit=4)
    return forward[None], backward[None]


def solution(mesh):
    split = Mesh(np.asarray(mesh.devices).reshape(8, 4, 4, 2), ("z", "x", "y", "core"))
    row, col = ("z", "x"), ("y", "core")
    return jax.shard_map(
        per_device,
        mesh=split,
        in_specs=(P(None, row, None), P(col, row, None), P(col, row, None)),
        out_specs=(P(col, None, None), P(col, None, row, None)),
        check_vma=False,
    )
```

```python
import functools

import jax
import jax.numpy as jnp
import numpy as np
from jax import lax
from jax.experimental import pallas as pl
from jax.experimental.pallas import tpu as pltpu
from jax.sharding import Mesh, PartitionSpec as P

SIZES = {"z": 8, "x": 4, "y": 4, "core": 2}
F32, BF16 = jnp.float32, jnp.bfloat16


def shift(value, axis, by):
    size = SIZES[axis]
    return lax.ppermute(value, axis, [(i, (i + by) % size) for i in range(size)])


def swap(value, axis, mask):
    return lax.ppermute(value, axis, [(i, i ^ mask) for i in range(SIZES[axis])])


def parts_of(value):
    high = value.astype(BF16)
    return high, (value - high.astype(F32)).astype(BF16)


def times(value, high, low, dims):
    count = value.shape[0]
    vh, vl = parts_of(value)
    dot = functools.partial(lax.dot_general, dimension_numbers=((dims, ((), ()))), preferred_element_type=F32)
    main = dot(jnp.concatenate([vh, vl], axis=0), high)
    return main[:count] + (main[count:] + dot(vh, low))


def mm(value, matrix):
    return times(value, *matrix, ((1,), (0,)))


def mmt(value, matrix):
    return times(value, *matrix, ((1,), (1,)))


def whole(ref, columns):
    return ref[0, :, columns], ref[1, :, columns]


def rows_of_a(refs):
    order = [(0, 64), (64, 64), (128, 64), (192, 64), (256, 32), (288, 32), (320, 64), (384, 64), (448, 64)]
    return [(start, size, ref) for (start, size), ref in zip(order, refs)]


def rows_of_b(refs):
    return [(s * 64 + k * 16, s, ref) for k, ref in enumerate(refs) for s in range(8)]


def put_parts(mat, rows, columns, value):
    high, low = parts_of(value)
    mat[0, rows, columns] = high
    mat[1, rows, columns] = low


def pack_kernel(place, right, off, diag, b_out, *a_outs):
    b_out[:, 1536:1664] = off[:, 0:128]
    b_out[:, 1664:1792] = diag[:, 64:192]
    b_out[:, 1792:1856] = diag[:, 0:64]
    b_out[:, 0:768] = diag[:, 192:960]
    b_out[:, 768:1536] = off[:, 128:896]
    x, core = place[1], place[3]
    column = 2 * place[2] + core
    for k in range(4):
        out = a_outs[k]
        at = pl.ds(pl.multiple_of(lax.rem(x + k, 4) * 128, 128), 128)
        out[:, 0:1280] = off[:, 896:2176]
        out[:, 1280:1408] = right[7 + column, :, at]
        for m in (2, 1, 0):
            both = right[2**m - 1 + lax.shift_right_logical(column, 3 - m), :, at]
            to = 1408 + 64 * (2 - m)
            out[:, to:to + 64] = jnp.where(core == 0, both[:, 0:64], both[:, 64:128])


def column_blocks_kernel(*refs):
    main, low = refs[8], refs[9]
    size = 16
    for first, ref in zip(range(0, 128, 16), refs):
        main[first // 16, :, :] = ref[:, 0:1536]
        low[first:first + size, :] = ref[:, 1536:1664]
        low[128 + first:128 + first + size, :] = ref[:, 1664:1792]
        at = first // 64 * 64
        low[256 + first % 64:256 + first % 64 + size, at:at + 64] = ref[:, 1792:1856]


def pair_kernel(own, other, out):
    for i, ref in enumerate((own, other)):
        out[0:64, 64 * i:64 * i + 64] = ref[256:320, 0:64]
        out[64:128, 64 * i:64 * i + 64] = ref[256:320, 64:128]


def slab_kernel(own, other, pair, far, out):
    out[:, 0:128] = own[0:128]
    out[:, 128:256] = other[0:128]
    out[:, 256:384] = own[128:256]
    out[:, 384:512] = other[128:256]
    out[:, 512:640] = pair[...]
    out[:, 640:768] = far[...]


def low_rows_kernel(b0, b1, b2, b2_low, b3, out):
    for k, refs in enumerate(((b0,), (b1,), (b2, b2_low), (b3,))):
        for s in range(8):
            ref, at = refs[s // 4 if len(refs) > 1 else 0], 16 * (s % 4 if len(refs) > 1 else s)
            out[s * 64 + k * 16:s * 64 + k * 16 + 16, :] = ref[at:at + 16, :]


def mine_kernel(*refs):
    out = refs[4]
    for start, s, ref in rows_of_b(refs[:4]):
        out[start:start + 16, 0:256] = ref[s, :, 0:256]
        out[start:start + 16, 256:768] = ref[s, :, 768:1280]


def level3_kernel(place, *refs):
    a_refs, b_refs = rows_of_a(refs[:9]), rows_of_b(refs[9:13])
    mat, keep, y3_out, kept_out, given_out, b2t_out, rhs, up = refs[13:]
    for start, size, ref in a_refs:
        rhs[start:start + size, 0:320] = ref[:, 1280:1600]
        put_parts(mat, slice(start, start + size), slice(256, 1536), ref[:, 0:1280])
    for start, s, ref in b_refs:
        put_parts(mat, slice(start, start + 16), slice(1536, 2048), ref[s, :, 256:768])
        put_parts(mat, slice(start, start + 16), slice(0, 256), ref[s, :, 1280:1536])
    rhs[:, 320:384] = jnp.zeros((512, 64), F32)
    b3t = rhs[:, 0:128].T
    b21t = rhs[:, 128:256].T
    b2t_out[...] = b21t[0:64]
    keep[128:192] = b21t[64:128]
    keep[192:256] = rhs[:, 256:384].T[0:64]
    y3t = mm(b3t, whole(mat, slice(1536, 2048)))
    keep[0:128] = y3t
    y3_out[...] = y3t.T
    for at, column in ((0, 1024), (512, 512), (1024, 0)):
        up[:, at:at + 512] = mmt(y3t, whole(mat, slice(column, column + 512)))
    core = place[3]
    kept_out[...] = up[pl.ds(pl.multiple_of(64 * core, 64), 64), :]
    given_out[...] = up[pl.ds(pl.multiple_of(64 * (1 - core), 64), 64), :]


def level2_kernel(mine, theirs, kept, got, b2t, mat, y2t_out, up_out):

    @pl.loop(0, 8)
    def _(s):
        at = pl.ds(pl.multiple_of(64 * s, 64), 64)
        for i in range(3):
            for j, ref in ((0, mine), (256, theirs)):
                put_parts(mat, at, slice(512 * i + j, 512 * i + j + 256), ref[at, 256 * i:256 * i + 256])

    up3 = kept[...] + got[...]
    y2t = mm(b2t[...] - up3[:, 0:512], whole(mat, slice(0, 512)))
    y2t_out[...] = y2t
    up_out[:, 0:512] = up3[:, 512:1024] + mmt(y2t, whole(mat, slice(1024, 1536)))
    up_out[:, 512:1024] = up3[:, 1024:1536] + mmt(y2t, whole(mat, slice(512, 1024)))


def low_matrices_kernel(mine, theirs, mat):
    @pl.loop(0, 8)
    def _(s):
        at = pl.ds(pl.multiple_of(64 * s, 64), 64)
        for i in range(3):
            for j, ref in ((0, mine), (256, theirs)):
                put_parts(mat, at, slice(512 * i + j, 512 * i + j + 256), ref[at, 256 * i:256 * i + 256])


def level1_kernel(up_ref, got, y2t, mat, keep, y1t_out, up_out, give_out):
    y1t = mm(keep[128:192] - (up_ref[:, 0:512] + got[:, 0:512]), whole(mat, slice(512, 1024)))
    y1t_out[...] = y1t
    up_out[...] = (up_ref[:, 512:1024] + got[:, 512:1024]) + mmt(y1t, whole(mat, slice(0, 512)))
    give_out[:, 0:128] = y1t[:, 256:384]
    give_out[:, 128:384] = y2t[:, 256:512]


def level0_kernel(up_ref, got, y2t, y1t, mat2, mat, keep, y0t_out, low_out):
    d2, l02, l12 = (whole(mat2, slice(512 * i, 512 * i + 512)) for i in range(3))
    l01, d1, d0 = (whole(mat, slice(512 * i, 512 * i + 512)) for i in range(3))
    y0t = mm(keep[192:256] - (up_ref[...] + got[...]), d0)
    y0t_out[...] = y0t
    low_out[:, 1536:1600] = y0t[:, 256:320]
    x0t = mmt(y0t, d0)
    low_out[:, 0:512] = x0t
    x1t = mmt(y1t[...] - mm(x0t, l01), d1)
    low_out[:, 512:1024] = x1t
    low_out[:, 1024:1536] = mmt(y2t[...] - mm(x0t, l02) - mm(x1t, l12), d2)


def halves(place):
    core = place[3]
    return pl.ds(pl.multiple_of(64 * core, 64), 64), pl.ds(pl.multiple_of(64 * (1 - core), 64), 64)


def rows_kernel(place, y1t, y2t, got, out, both):
    here, there = halves(place)
    both[here, 0:128] = y1t[:, 0:128]
    both[here, 128:384] = y2t[:, 0:256]
    both[there, :] = got[...]
    out[...] = both[...].T


def last_kernel(place, low, got, y0t, keep, mat, *refs):
    outs, both, tops = refs[:4], refs[4], refs[5]
    here, there = halves(place)
    both[here, :] = low[:, 0:1536]
    both[there, :] = got[:, 0:1536]
    tops[here, 0:64] = y0t[:, 0:64]
    tops[there, 0:64] = got[:, 1536:1600]
    rest = keep[0:128]
    for k in range(3):
        rest = rest - mm(both[:, 512 * k:512 * k + 512], whole(mat, slice(512 * k, 512 * k + 512)))
        tops[:, 64 * k + 64:64 * k + 128] = both[:, 512 * k:512 * k + 64]
    tops[:, 256:320] = mmt(rest, (mat[0, 0:64, 1536:2048], mat[1, 0:64, 1536:2048]))
    tops[:, 320:384] = jnp.zeros((128, 64), F32)
    rows = tops[...].T
    for k in range(4):
        outs[k][0:64, :] = rows[0:64]
        for n in range(4):
            at = 64 + 64 * n + 16 * ((4 - k) % 4)
            outs[k][64 + 16 * n:80 + 16 * n, :] = rows[at:at + 16]


def forward_kernel(place, p0, p1, p2, p3, out):
    for k, ref in enumerate((p0, p1, p2, p3)):
        at = pl.ds(pl.multiple_of(lax.rem(place[1] + 4 - k, 4) * 128, 128), 128)
        out[0:448, at] = jnp.zeros((448, 128), F32)
        out[448:960, at] = ref[...]


def final_kernel(place, m0, m1, m2, m3, r0, r1, r2, r3, forward_in, forward_out, x_hbm, top, x_out, sems):
    del forward_in
    for k, (ref, rows) in enumerate(((m0, r0), (m1, r1), (m2, r2), (m3, r3))):
        at = pl.ds(pl.multiple_of(lax.rem(place[1] + 4 - k, 4) * 128, 128), 128)
        top[0:64, at] = ref[0:64, :]
        top[64:448, at] = rows[...]
        for n in range(4):
            x_out[n, :, at] = ref[64 + 16 * n:80 + 16 * n, :]
    copies = (pltpu.make_async_copy(top, forward_out.at[0:448], sems.at[0]), pltpu.make_async_copy(x_out, x_hbm, sems.at[1]))
    for copy in copies:
        copy.start()
    for copy in copies:
        copy.wait()


VMEM, SMEM, ANY = (pl.BlockSpec(memory_space=m) for m in (pltpu.VMEM, pltpu.SMEM, pl.ANY))


def call(kernel, name, outs, *args, scalars=1, scratch=(), in_specs=None, out_specs=None, aliases=None, limit=6):
    return pl.pallas_call(
        kernel,
        name=name,
        out_shape=[jax.ShapeDtypeStruct(shape, kind) for shape, kind in outs],
        in_specs=in_specs or [SMEM] * scalars + [VMEM] * (len(args) - scalars),
        out_specs=out_specs or [VMEM] * len(outs),
        scratch_shapes=list(scratch),
        input_output_aliases=aliases or {},
        compiler_params=pltpu.CompilerParams(vmem_limit_bytes=limit * 2**20),
    )(*args)


def after(value, *others):
    return lax.optimization_barrier((value,) + others)[0]


def per_device(right_side, off_blocks, diag_inverse):
    place = jnp.stack([lax.axis_index(a) for a in ("z", "x", "y", "core")]).astype(jnp.int32)

    stream_b, *stream_a = call(
        pack_kernel, "pack", [((16, 1856), F32)] + [((16, 1600), F32)] * 4,
        place, right_side, off_blocks[0], diag_inverse[0], limit=8)

    wait = lax.optimization_barrier

    def both_ways(up, down, axis):
        return shift(up, axis, 1), shift(down, axis, -1)

    b1 = both_ways(stream_b, stream_b, "z")
    *b1, a_1, a_2, a_3, far_b = wait((*b1, *stream_a[1:], stream_b))
    b2 = both_ways(*b1, "z")
    b4 = shift(far_b, "z", 4)
    across = [shift(a_1, "x", 1), shift(a_2, "x", 2), shift(a_3, "x", 3)]
    b3 = both_ways(*b2, "z")
    b4, *b3, across1, across2, across3 = wait((b4, *b3, *across))
    block_a = jnp.concatenate([stream_a[0], across1, across2, across3], axis=0)
    a1 = both_ways(block_a, block_a, "z")
    main, low = call(column_blocks_kernel, "column_blocks", [((8, 16, 1536), F32), ((320, 128), F32)],
                     stream_b, b1[0], b2[0], b3[0], b4, b3[1], b2[1], b1[1], scalars=0)
    c1_up, c1_down = both_ways(main, main, "x")
    other = swap(low, "y", 1)
    other, a1_up, a1_down = wait((other, *a1))
    a2 = both_ways(a1_up, a1_down, "z")
    (pair,) = call(pair_kernel, "pair", [((128, 128), F32)], low, other, scalars=0)
    far = swap(pair, "y", 2)
    c2 = shift(c1_up, "x", 1)
    a2_up, a2_down, far, c1_down = wait((*a2, far, c1_down))
    a3 = both_ways(a2_up, a2_down, "z")
    (slab,) = call(slab_kernel, "slab", [((128, 768), F32)], low, other, pair, far, scalars=0)
    e1 = both_ways(slab, slab, "x")
    e1_up, e1_down = e1
    a3_up, a3_down, e1_down = wait((*a3, e1_down))
    a4 = both_ways(a3_up[:32], a3_down[32:], "z")
    e2 = both_ways(e1_up[:64], e1_down[64:], "x")
    *a4, c2, e1_up, e2_up, e2_down = wait((*a4, c2, e1_up, *e2))
    blocks_b = [main, c1_up, c2, c1_down]
    blocks_a = [block_a, a1_up, a2_up, a3_up, a4[0], a4[1], a3_down, a2_down, a1_down]

    (mine,) = call(mine_kernel, "mine", [((512, 768), F32)], *blocks_b, scalars=0, limit=6)
    theirs = swap(mine, "core", 1)

    mat3, keep, y3, kept, given, b2t = call(
        level3_kernel, "level3",
        [((2, 512, 2048), BF16), ((256, 512), F32), ((512, 128), F32), ((64, 1536), F32), ((64, 1536), F32),
         ((64, 512), F32)],
        place, *blocks_a, *blocks_b,
        scratch=[pltpu.VMEM((512, 384), F32), pltpu.VMEM((128, 1536), F32)])
    got = swap(given, "core", 1)
    slab, _ = wait((slab, given))
    (low_mine,) = call(low_rows_kernel, "low_rows", [((512, 768), F32)], slab, e1_up, e2_up, e2_down, e1_down, scalars=0)
    mat2, y2t, up = call(
        level2_kernel, "level2", [((2, 512, 1536), BF16), ((64, 512), F32), ((64, 1024), F32)],
        mine, theirs, kept, got, b2t, scalars=0)
    got = swap(up, "y", 1)
    low_theirs = swap(wait((low_mine, up))[0], "core", 1)
    y3 = after(y3, up)
    top_parts = [y3] + [shift(y3, "x", k) for k in (1, 2, 3)]
    (mat1,) = call(low_matrices_kernel, "low_matrices", [((2, 512, 1536), BF16)], low_mine, low_theirs, scalars=0)
    y1t, up, give = call(
        level1_kernel, "level1", [((64, 512), F32), ((64, 512), F32), ((64, 384), F32)],
        up, got, y2t, mat1, keep, scalars=0)
    got = swap(up, "y", 2)
    (rows,) = call(rows_kernel, "rows", [((384, 128), F32)], place, y1t, y2t, swap(give, "core", 1),
                   scratch=[pltpu.VMEM((128, 384), F32)], limit=4)
    got = after(got, rows, *top_parts)
    mid_parts = [rows] + [shift(rows, "x", k) for k in (1, 2, 3)]
    y0t, low = call(level0_kernel, "level0", [((64, 512), F32), ((64, 1600), F32)],
                    up, got, y2t, y1t, mat2, mat1, keep, scalars=0)

    messages = call(last_kernel, "last", [((128, 128), F32)] * 4, place, low, swap(low, "core", 1), y0t, keep, mat3,
                    scratch=[pltpu.VMEM((128, 1536), F32), pltpu.VMEM((128, 384), F32)])
    held = wait(tuple(top_parts) + (messages[0],))[:4]
    (forward,) = call(forward_kernel, "forward", [((960, 512), F32)], place, *held, limit=8)
    arrived = [messages[0]] + [shift(messages[k], "x", k) for k in (1, 2, 3)]
    forward, backward = call(
        final_kernel, "final", [((960, 512), F32), ((4, 16, 512), F32)],
        place, *arrived, *mid_parts, forward,
        in_specs=[SMEM] + [VMEM] * 8 + [ANY], out_specs=[ANY, ANY], aliases={9: 0},
        scratch=[pltpu.VMEM((448, 512), F32), pltpu.VMEM((4, 16, 512), F32), pltpu.SemaphoreType.DMA((2,))], limit=4)
    return forward[None], backward[None]


def solution(mesh):
    split = Mesh(np.asarray(mesh.devices).reshape(8, 4, 4, 2), ("z", "x", "y", "core"))
    row, col = ("z", "x"), ("y", "core")
    return jax.shard_map(
        per_device,
        mesh=split,
        in_specs=(P(None, row, None), P(col, row, None), P(col, row, None)),
        out_specs=(P(col, None, None), P(col, None, row, None)),
        check_vma=False,
    )
```
